256 devices in a mesh: slab: 8 (over z), filt: 32 (over y, x, core).
Axes of the slice: x: 4, y: 4, z: 8, core: 2. Of those that a mesh axis runs over, the one named last changes fastest.
Arguments:
- features: bfloat16 [32, 256, 64, 128], P('slab', 'filt'), may hold values from -6 to 6
- kernel: bfloat16 [3, 3, 3, 256, 256], P(None, None, None, 'filt'), may hold values from -0.078125 to 0.078125
- bias_vector: float32 [256], replicated, may hold values from -0.6 to 0.6
Outputs:
- activated: bfloat16 [32, 256, 64, 128], P('slab', 'filt')
The draws below stay inside these ranges and needn't reach their ends.
All inputs are finite; a program needn't handle non-finite values.
Results may differ from the reference program's by a relative error of at most 0.005.
Values may be sent and summed in bfloat16 or wider, within the bound.
A program may use at most 128 MiB of HBM per device.

```python
import jax
import jax.numpy as jnp
from jax import lax

CIN = 256
COUT = 256
Y = 64
X = 128
Z = 32


def block_levels(key, extent, pieces, low, largest):
    factor_of = 1.0
    for dim, blocks in pieces:
        draws = jax.random.uniform(jax.random.fold_in(jax.random.fold_in(key, 6), dim), (blocks,), jnp.float32, low / len(pieces), largest / len(pieces))
        factor_of = factor_of * jnp.repeat(jnp.exp(draws), extent[dim] // blocks).reshape((-1,) + (1,) * (len(extent) - 1 - dim))
    return factor_of


def centred(key, extent, scale, limit, pieces=(), kind=jnp.bfloat16):
    loudness = block_levels(key, extent, pieces, -0.22, 0.18) if pieces else 1.0
    entries = jax.random.normal(key, extent, jnp.float32) * scale * loudness
    return jnp.minimum(jnp.maximum(entries, -limit), limit).astype(kind)


def setup_inputs(seed: int = 0) -> dict:
    key_list = jax.random.split(jax.random.key(seed), 4)
    features = centred(key_list[0], (Z, CIN, Y, X), 1.0, 6.0, ((0, 8), (1, 32)))
    kernel = centred(key_list[1], (3, 3, 3, COUT, CIN), (27 * CIN) ** -0.5, 0.078125, ((3, 32),))
    bias_vector = jnp.clip(jax.random.uniform(key_list[2], (COUT,), jnp.float32, -0.6, 0.6), -0.6, 0.6)
    return dict(features=features, kernel=kernel, bias_vector=bias_vector)


def reference(features, kernel, bias_vector):
    volume = features.astype(jnp.float32).transpose(1, 0, 2, 3)[None]
    filters = kernel.astype(jnp.float32).transpose(3, 4, 0, 1, 2)
    convolved = lax.conv_general_dilated(volume, filters, (1, 1, 1), ((1, 1), (1, 1), (1, 1)), dimension_numbers=("NCDHW", "OIDHW", "NCDHW"), precision=lax.Precision.HIGHEST)
    shifted = convolved[0].transpose(1, 0, 2, 3) + bias_vector[None, :, None, None]
    return jnp.where(shifted > 0, shifted, 0.3 * shifted).astype(jnp.bfloat16)
```

```python
import jax
import jax.numpy as jnp
from jax import lax
from jax.experimental import pallas as pl
from jax.experimental.pallas import tpu as pltpu
from jax.sharding import PartitionSpec as P

MESH = pl.DeviceIdType.MESH
SIDE = 4
CHIPS = 16
ROWS = 4
PLANES = 4
ORDER = [3, 4, 5, 0, 1, 2, 6, 7, 8]


def kernel(feat, w, bias, out, turned, vol, taps, acc, ready, column,
           f_s, f_r, x_s, x_r, h_s, h_r, w1_s, w1_r, w2_s, w2_r, o_s, o_r, l_s):
    slab = lax.axis_index("slab")
    filt = lax.axis_index("filt")
    slabs = lax.axis_size("slab")
    chip = filt // 2
    core = filt % 2
    cy = chip // SIDE
    cx = chip % SIDE

    def device(y, x, c):
        return {"filt": (y * SIDE + x) * 2 + c}

    def partner(k):
        y = (cy + k // SIDE) % SIDE
        x = (cx + k % SIDE) % SIDE
        return y, x

    def source(k):
        y = (cy + SIDE - k // SIDE) % SIDE
        x = (cx + SIDE - k % SIDE) % SIDE
        return y * SIDE + x

    barrier = pltpu.get_barrier_semaphore()

    def greet(k, carry):
        y, x = partner(k)
        pl.semaphore_signal(barrier, inc=1, device_id=device(y, x, core), device_id_type=MESH)
        return carry

    lax.fori_loop(1, CHIPS, greet, 0)
    pl.semaphore_signal(barrier, inc=1, device_id=device(cy, cx, 1 - core), device_id_type=MESH)

    for step in (1, slabs - 1):
        pl.semaphore_signal(
            barrier, inc=1, device_id={"slab": (slab + step) % slabs}, device_id_type=MESH
        )

    own_taps = pltpu.make_async_copy(w, taps.at[:, :, cy, cx], l_s.at[0])
    own_taps.start()

    turned[0] = jnp.zeros(turned.shape[1:], turned.dtype)
    turned[turned.shape[0] - 1] = jnp.zeros(turned.shape[1:], turned.dtype)
    for z in range(PLANES):
        turned[1:65, z] = jnp.transpose(feat[z].astype(jnp.float32), (1, 0, 2)).astype(jnp.bfloat16)

    own_feat = pltpu.make_async_copy(
        turned.at[pl.ds(chip * ROWS, ROWS + 2)], vol.at[:, 1:5, chip, core], l_s.at[1]
    )
    own_feat.start()

    wide = jnp.broadcast_to(bias[...].reshape(1, 256), (128, 256))
    column[...] = jnp.transpose(wide, (1, 0)).reshape(CHIPS, 2, 8, 128)

    pl.semaphore_wait(barrier, CHIPS + 2)

    def feat_copy(k):
        y, x = partner(k)
        return pltpu.make_async_remote_copy(
            src_ref=turned.at[pl.ds((y * SIDE + x) * ROWS, ROWS + 2)],
            dst_ref=vol.at[:, 1:5, chip, core],
            send_sem=f_s.at[k], recv_sem=f_r.at[k],
            device_id=device(y, x, core), device_id_type=MESH,
        )

    def feat_arrived(k):
        piece = vol.at[:, 1:5, source(k), core]
        return pltpu.make_async_copy(piece, piece, f_r.at[k])

    def send_feat(k, carry):
        feat_copy(k).start()
        return carry

    lax.fori_loop(1, CHIPS, send_feat, 0)

    def ring(unit, k, phase):
        along_x = (unit % 2 == 0) == (phase == 1)
        if along_x:
            return cy, (cx + k) % SIDE
        return (cy + k) % SIDE, cx

    def ring_source(unit, k, phase):
        along_x = (unit % 2 == 0) == (phase == 1)
        if along_x:
            return cy, (cx + SIDE - k) % SIDE
        return (cy + SIDE - k) % SIDE, cx

    def tap_copy1(unit, k):
        y, x = ring(unit, k, 1)
        return pltpu.make_async_remote_copy(
            src_ref=w.at[unit], dst_ref=taps.at[unit, :, cy, cx],
            send_sem=w1_s.at[unit, k], recv_sem=w1_r.at[unit, k],
            device_id=device(y, x, core), device_id_type=MESH,
        )

    def tap_arrived1(unit, k):
        y, x = ring_source(unit, k, 1)
        piece = taps.at[unit, :, y, x]
        return pltpu.make_async_copy(piece, piece, w1_r.at[unit, k])

    def tap_line(unit, y, x):
        if unit % 2 == 0:
            return taps.at[unit, :, y]
        return taps.at[unit, :, :, x]

    def tap_copy2(unit, k):
        y, x = ring(unit, k, 2)
        line = tap_line(unit, cy, cx)
        return pltpu.make_async_remote_copy(
            src_ref=line, dst_ref=line,
            send_sem=w2_s.at[unit, k], recv_sem=w2_r.at[unit, k],
            device_id=device(y, x, core), device_id_type=MESH,
        )

    def tap_arrived2(unit, k):
        y, x = ring_source(unit, k, 2)
        line = tap_line(unit, y, x)
        return pltpu.make_async_copy(line, line, w2_r.at[unit, k])

    for unit in ORDER:
        for k in range(1, SIDE):
            tap_copy1(unit, k).start()

    own_feat.wait()

    def wait_feat(k, carry):
        feat_arrived(k).wait()
        return carry

    lax.fori_loop(1, CHIPS, wait_feat, 0)

    def across(index, part):
        return pltpu.make_async_remote_copy(
            src_ref=part, dst_ref=part, send_sem=x_s.at[index], recv_sem=x_r.at[index],
            device_id=device(cy, cx, 1 - core), device_id_type=MESH,
        )

    def across_arrived(index, part):
        return pltpu.make_async_copy(part, part, x_r.at[index])

    down = pltpu.make_async_remote_copy(
        src_ref=vol.at[:, 1, :, core], dst_ref=vol.at[:, 5, :, core],
        send_sem=h_s.at[0], recv_sem=h_r.at[0],
        device_id={"slab": slab - 1}, device_id_type=MESH,
    )
    up = pltpu.make_async_remote_copy(
        src_ref=vol.at[:, 4, :, core], dst_ref=vol.at[:, 0, :, core],
        send_sem=h_s.at[1], recv_sem=h_r.at[1],
        device_id={"slab": slab + 1}, device_id_type=MESH,
    )

    @pl.when(slab > 0)
    def _():
        down.start()

    @pl.when(slab < slabs - 1)
    def _():
        up.start()

    middle = across(0, vol.at[:, 1:5, :, core])
    middle.start()

    @pl.when(slab == 0)
    def _():
        for y in range(ROWS + 2):
            vol[y, 0] = jnp.zeros(vol.shape[2:], vol.dtype)

    @pl.when(slab == slabs - 1)
    def _():
        for y in range(ROWS + 2):
            vol[y, 5] = jnp.zeros(vol.shape[2:], vol.dtype)

    own_taps.wait()
    for unit in ORDER:
        for k in range(1, SIDE):
            tap_arrived1(unit, k).wait()
        for k in range(1, SIDE):
            tap_copy2(unit, k).start()

    low = across(1, vol.at[:, 0, :, core])
    high = across(2, vol.at[:, 5, :, core])

    @pl.when(slab > 0)
    def _():
        edge = vol.at[:, 0, :, core]
        pltpu.make_async_copy(edge, edge, h_r.at[1]).wait()
        low.start()

    @pl.when(slab < slabs - 1)
    def _():
        edge = vol.at[:, 5, :, core]
        pltpu.make_async_copy(edge, edge, h_r.at[0]).wait()
        high.start()

    across_arrived(0, vol.at[:, 1:5, :, 1 - core]).wait()

    lane = lax.broadcasted_iota(jnp.int32, (128, 128), 1)

    def out_copy(z, k):
        y, x = partner(k)
        return pltpu.make_async_remote_copy(
            src_ref=ready.at[z, y * SIDE + x], dst_ref=out.at[z, pl.ds(chip * ROWS, ROWS)],
            send_sem=o_s.at[z, k], recv_sem=o_r.at[z, k],
            device_id=device(y, x, core), device_id_type=MESH,
        )

    def out_arrived(z, k):
        piece = out.at[z, pl.ds(source(k) * ROWS, ROWS)]
        return pltpu.make_async_copy(piece, piece, o_r.at[z, k])

    def out_own(z):
        return pltpu.make_async_copy(
            ready.at[z, chip], out.at[z, pl.ds(chip * ROWS, ROWS)], o_s.at[z, 0]
        )

    def finish(z):
        biases = column[:, core].reshape(128, 128)
        for y in range(ROWS):
            part = acc[z, :, y * 128 : (y + 1) * 128]
            before = jnp.where(lane == 0, 0.0, pltpu.roll(part[0:128], 1, 1))
            after = jnp.where(lane == 127, 0.0, pltpu.roll(part[256:384], 127, 1))
            shifted = before + part[128:256] + after + biases
            active = jnp.where(shifted > 0, shifted, 0.3 * shifted)
            ready[z, :, y] = active.reshape(CHIPS, 8, 128).astype(jnp.bfloat16)
        out_own(z).start()

        def send(k, carry):
            out_copy(z, k).start()
            return carry

        lax.fori_loop(1, CHIPS, send, 0)

    for unit in ORDER:
        dz, dy = unit // 3, unit % 3
        if unit == ORDER[3]:
            @pl.when(slab > 0)
            def _():
                across_arrived(1, vol.at[:, 0, :, 1 - core]).wait()

            @pl.when(slab < slabs - 1)
            def _():
                across_arrived(2, vol.at[:, 5, :, 1 - core]).wait()
        for k in range(1, SIDE):
            tap_arrived2(unit, k).wait()

        def plane(z, carry, unit=unit, dz=dz, dy=dy):
            weight = taps[unit].reshape(384, 256)
            lines = [vol[dy + y, z + dz].reshape(256, 128) for y in range(ROWS)]
            product = jnp.dot(weight, jnp.concatenate(lines, axis=1), preferred_element_type=jnp.float32)
            if unit == ORDER[0]:
                acc[z] = product
            else:
                acc[z] += product
            if unit == ORDER[8]:
                finish(z)
            return carry

        lax.fori_loop(0, PLANES, plane, 0)

    def drain_out(i, carry):
        z = i // CHIPS
        k = i % CHIPS

        @pl.when(k == 0)
        def _():
            out_own(z).wait()

        @pl.when(k > 0)
        def _():
            out_copy(z, k).wait_send()
            out_arrived(z, k).wait()

        return carry

    lax.fori_loop(0, PLANES * CHIPS, drain_out, 0)

    def drain_feat(k, carry):
        feat_copy(k).wait_send()
        return carry

    lax.fori_loop(1, CHIPS, drain_feat, 0)
    for unit in ORDER:
        for k in range(1, SIDE):
            tap_copy1(unit, k).wait_send()
            tap_copy2(unit, k).wait_send()
    middle.wait_send()

    @pl.when(slab > 0)
    def _():
        down.wait_send()
        low.wait_send()

    @pl.when(slab < slabs - 1)
    def _():
        up.wait_send()
        high.wait_send()


def body(features, weights, bias_vector):
    DMA = pltpu.SemaphoreType.DMA
    vmem = pl.BlockSpec(memory_space=pltpu.VMEM)
    anywhere = pl.BlockSpec(memory_space=pl.ANY)
    flat = weights.reshape(9, 3, 8, 256)
    got = pl.pallas_call(
        kernel,
        out_shape=jax.ShapeDtypeStruct((PLANES, 64, 8, 128), jnp.bfloat16),
        in_specs=[vmem, anywhere, vmem],
        out_specs=anywhere,
        scratch_shapes=[
            pltpu.VMEM((66, PLANES, 8, 128), jnp.bfloat16),
            pltpu.VMEM((ROWS + 2, PLANES + 2, CHIPS, 2, 8, 128), jnp.bfloat16),
            pltpu.VMEM((9, 3, SIDE, SIDE, 8, 256), jnp.bfloat16),
            pltpu.VMEM((PLANES, 384, ROWS * 128), jnp.float32),
            pltpu.VMEM((PLANES, CHIPS, ROWS, 8, 128), jnp.bfloat16),
            pltpu.VMEM((CHIPS, 2, 8, 128), jnp.float32),
            DMA((CHIPS,)), DMA((CHIPS,)),
            DMA((3,)), DMA((3,)),
            DMA((2,)), DMA((2,)),
            DMA((9, SIDE)), DMA((9, SIDE)),
            DMA((9, SIDE)), DMA((9, SIDE)),
            DMA((PLANES, CHIPS)), DMA((PLANES, CHIPS)),
            DMA((2,)),
        ],
        compiler_params=pltpu.CompilerParams(
            collective_id=0, has_side_effects=True, vmem_limit_bytes=40 * 1024 * 1024
        ),
    )(features, flat, bias_vector)
    return got.transpose(0, 2, 1, 3)


def solution(mesh):
    placed = (P("slab", "filt", None, None), P(None, None, None, "filt", None), P())
    return jax.shard_map(
        body, mesh=mesh, in_specs=placed, out_specs=P("slab", "filt", None, None), check_vma=False
    )
```

```python
import jax
import jax.numpy as jnp
from jax import lax
from jax.experimental import pallas as pl
from jax.experimental.pallas import tpu as pltpu
from jax.sharding import PartitionSpec as P

MESH = pl.DeviceIdType.MESH
SIDE = 4
CHIPS = 16
ROWS = 4
PLANES = 4
COUPLES = ()
COMMON = (3, 4, 5, 1, 7, 0, 2, 6, 8)
OWN = len(COUPLES) + len(COMMON)
X_FIRST = (0, 2, 4, 6, 8)


def kernel(feat_hbm, w, bias_hbm, out, feat, bias, turned, vol, taps, acc, ready, column,
           f_s, f_r, x_s, x_r, h_s, h_r, w1_s, w1_r, w2_s, w2_r, z_s, z_r, o_s, o_r, l_s):
    slab = lax.axis_index("slab")
    filt = lax.axis_index("filt")
    slabs = lax.axis_size("slab")
    chip = filt // 2
    core = filt % 2
    cy = chip // SIDE
    cx = chip % SIDE

    def device(y, x, c):
        return {"filt": (y * SIDE + x) * 2 + c}

    def partner(k):
        y = (cy + k // SIDE) % SIDE
        x = (cx + k % SIDE) % SIDE
        return y, x

    def source(k):
        y = (cy + SIDE - k // SIDE) % SIDE
        x = (cx + SIDE - k % SIDE) % SIDE
        return y * SIDE + x

    barrier = pltpu.get_barrier_semaphore()

    def greet(k, carry):
        y, x = partner(k)
        pl.semaphore_signal(barrier, inc=1, device_id=device(y, x, core), device_id_type=MESH)
        return carry

    lax.fori_loop(1, CHIPS, greet, 0)
    pl.semaphore_signal(barrier, inc=1, device_id=device(cy, cx, 1 - core), device_id_type=MESH)

    for step in (1, slabs - 1):
        pl.semaphore_signal(
            barrier, inc=1, device_id={"slab": (slab + step) % slabs}, device_id_type=MESH
        )

    odd = slab % 2

    def pair(i, parity):
        if i >= len(COUPLES):
            return COMMON[i - len(COUPLES)]
        first, second = COUPLES[i]
        return first + parity * (second - first)

    take_feat = pltpu.make_async_copy(feat_hbm, feat, l_s.at[0])
    take_feat.start()
    take_bias = pltpu.make_async_copy(bias_hbm, bias, l_s.at[1])
    take_bias.start()
    own_taps = []
    for i in range(OWN):
        unit = pair(i, odd)
        own_taps.append(pltpu.make_async_copy(w.at[unit], taps.at[unit, :, cy, cx], l_s.at[3 + i]))
        own_taps[i].start()

    @pl.when(slab == 0)
    def _():
        for y in range(ROWS + 2):
            vol[y, 0] = jnp.zeros(vol.shape[2:], vol.dtype)

    @pl.when(slab == slabs - 1)
    def _():
        for y in range(ROWS + 2):
            vol[y, 5] = jnp.zeros(vol.shape[2:], vol.dtype)

    turned[0] = jnp.zeros(turned.shape[1:], turned.dtype)
    turned[turned.shape[0] - 1] = jnp.zeros(turned.shape[1:], turned.dtype)
    take_feat.wait()
    for z in range(PLANES):
        turned[1:65, z] = jnp.transpose(feat[z].astype(jnp.float32), (1, 0, 2)).astype(jnp.bfloat16)

    own_feat = pltpu.make_async_copy(
        turned.at[pl.ds(chip * ROWS, ROWS + 2)], vol.at[:, 1:5, chip, core], l_s.at[2]
    )
    own_feat.start()

    take_bias.wait()
    wide = jnp.broadcast_to(bias[...].reshape(1, 256), (128, 256))
    column[...] = jnp.transpose(wide, (1, 0)).reshape(CHIPS, 2, 8, 128)

    pl.semaphore_wait(barrier, CHIPS + 2)

    def feat_copy(k):
        y, x = partner(k)
        return pltpu.make_async_remote_copy(
            src_ref=turned.at[pl.ds((y * SIDE + x) * ROWS, ROWS + 2)],
            dst_ref=vol.at[:, 1:5, chip, core],
            send_sem=f_s.at[k], recv_sem=f_r.at[k],
            device_id=device(y, x, core), device_id_type=MESH,
        )

    def feat_arrived(k):
        piece = vol.at[:, 1:5, source(k), core]
        return pltpu.make_async_copy(piece, piece, f_r.at[k])

    def send_feat(k, carry):
        feat_copy(k).start()
        return carry

    def ring(i, k, phase, sign):
        step = k if sign > 0 else SIDE - k
        if (i in X_FIRST) == (phase == 1):
            return cy, (cx + step) % SIDE
        return (cy + step) % SIDE, cx

    def tap_copy1(i, k):
        y, x = ring(i, k, 1, 1)
        return pltpu.make_async_remote_copy(
            src_ref=w.at[pair(i, odd)], dst_ref=taps.at[pair(i, odd), :, cy, cx],
            send_sem=w1_s.at[i, k], recv_sem=w1_r.at[i, k],
            device_id=device(y, x, core), device_id_type=MESH,
        )

    def tap_arrived1(i, k):
        y, x = ring(i, k, 1, -1)
        piece = taps.at[pair(i, odd), :, y, x]
        return pltpu.make_async_copy(piece, piece, w1_r.at[i, k])

    def tap_line(i, y, x):
        if i in X_FIRST:
            return taps.at[pair(i, odd), :, y]
        return taps.at[pair(i, odd), :, :, x]

    def tap_copy2(i, k):
        y, x = ring(i, k, 2, 1)
        line = tap_line(i, cy, cx)
        return pltpu.make_async_remote_copy(
            src_ref=line, dst_ref=line, send_sem=w2_s.at[i, k], recv_sem=w2_r.at[i, k],
            device_id=device(y, x, core), device_id_type=MESH,
        )

    def tap_arrived2(i, k):
        y, x = ring(i, k, 2, -1)
        line = tap_line(i, y, x)
        return pltpu.make_async_copy(line, line, w2_r.at[i, k])

    def tap_copy3(c):
        unit = taps.at[pair(c, odd)]
        step = 1 if c == 0 else slabs - 1
        return pltpu.make_async_remote_copy(
            src_ref=unit, dst_ref=unit, send_sem=z_s.at[c], recv_sem=z_r.at[c],
            device_id={"slab": (slab + step) % slabs}, device_id_type=MESH,
        )

    def tap_arrived3(c):
        unit = taps.at[pair(c, 1 - odd)]
        return pltpu.make_async_copy(unit, unit, z_r.at[c])

    def second_phase(which):
        for i in which:
            own_taps[i].wait()
            for k in range(1, SIDE):
                tap_arrived1(i, k).wait()
            for k in range(1, SIDE):
                tap_copy2(i, k).start()

    def third_phase():
        for c in range(len(COUPLES)):
            for k in range(1, SIDE):
                tap_arrived2(c, k).wait()
            tap_copy3(c).start()

    lax.fori_loop(1, CHIPS, send_feat, 0)
    for i in range(OWN):
        for k in range(1, SIDE):
            tap_copy1(i, k).start()
    second_phase(range(OWN))

    own_feat.wait()

    def wait_feat(k, carry):
        feat_arrived(k).wait()
        return carry

    lax.fori_loop(1, CHIPS, wait_feat, 0)

    def across(index, part):
        return pltpu.make_async_remote_copy(
            src_ref=part, dst_ref=part, send_sem=x_s.at[index], recv_sem=x_r.at[index],
            device_id=device(cy, cx, 1 - core), device_id_type=MESH,
        )

    def across_arrived(index, part):
        return pltpu.make_async_copy(part, part, x_r.at[index])

    down = pltpu.make_async_remote_copy(
        src_ref=vol.at[:, 1, :, core], dst_ref=vol.at[:, 5, :, core],
        send_sem=h_s.at[0], recv_sem=h_r.at[0],
        device_id={"slab": slab - 1}, device_id_type=MESH,
    )
    up = pltpu.make_async_remote_copy(
        src_ref=vol.at[:, 4, :, core], dst_ref=vol.at[:, 0, :, core],
        send_sem=h_s.at[1], recv_sem=h_r.at[1],
        device_id={"slab": slab + 1}, device_id_type=MESH,
    )

    @pl.when(slab > 0)
    def _():
        down.start()

    @pl.when(slab < slabs - 1)
    def _():
        up.start()

    middle = across(0, vol.at[:, 1:5, :, core])
    middle.start()
    third_phase()

    low = across(1, vol.at[:, 0, :, core])
    high = across(2, vol.at[:, 5, :, core])
    across_arrived(0, vol.at[:, 1:5, :, 1 - core]).wait()

    lane = lax.broadcasted_iota(jnp.int32, (128, 128), 1)

    def out_copy(z, k):
        y, x = partner(k)
        return pltpu.make_async_remote_copy(
            src_ref=ready.at[z, y * SIDE + x], dst_ref=out.at[z, pl.ds(chip * ROWS, ROWS)],
            send_sem=o_s.at[z, k], recv_sem=o_r.at[z, k],
            device_id=device(y, x, core), device_id_type=MESH,
        )

    def out_arrived(z, k):
        piece = out.at[z, pl.ds(source(k) * ROWS, ROWS)]
        return pltpu.make_async_copy(piece, piece, o_r.at[z, k])

    def out_own(z):
        return pltpu.make_async_copy(
            ready.at[z, chip], out.at[z, pl.ds(chip * ROWS, ROWS)], o_s.at[z, 0]
        )

    def finish(z):
        biases = column[:, core].reshape(128, 128)
        for y in range(ROWS):
            part = acc[z, :, y * 128 : (y + 1) * 128]
            before = jnp.where(lane == 0, 0.0, pltpu.roll(part[0:128], 1, 1))
            after = jnp.where(lane == 127, 0.0, pltpu.roll(part[256:384], 127, 1))
            shifted = before + part[128:256] + after + biases
            active = jnp.where(shifted > 0, shifted, 0.3 * shifted)
            ready[z, :, y] = active.reshape(CHIPS, 8, 128).astype(jnp.bfloat16)
        out_own(z).start()

        def send(k, carry):
            out_copy(z, k).start()
            return carry

        lax.fori_loop(1, CHIPS, send, 0)

    def multiply(unit, first=False, last=False):
        dz, dy = unit // 3, unit % 3
        lines = [
            vol[dy + y, z + dz].reshape(256, 128) for z in range(PLANES) for y in range(ROWS)
        ]
        product = jnp.dot(
            taps[unit].reshape(384, 256),
            jnp.concatenate(lines, axis=1),
            preferred_element_type=jnp.float32,
        )
        for z in range(PLANES):
            part = product[:, z * ROWS * 128 : (z + 1) * ROWS * 128]
            if first:
                acc[z] = part
            else:
                acc[z] += part
            if last:
                finish(z)

    for i in range(len(COUPLES), OWN):
        for k in range(1, SIDE):
            tap_arrived2(i, k).wait()
        if i == len(COUPLES) + 1:
            @pl.when(slab > 0)
            def _():
                edge = vol.at[:, 0, :, core]
                pltpu.make_async_copy(edge, edge, h_r.at[1]).wait()
                low.start()

            @pl.when(slab < slabs - 1)
            def _():
                edge = vol.at[:, 5, :, core]
                pltpu.make_async_copy(edge, edge, h_r.at[0]).wait()
                high.start()

        if i == len(COUPLES) + 3:
            @pl.when(slab > 0)
            def _():
                across_arrived(1, vol.at[:, 0, :, 1 - core]).wait()

            @pl.when(slab < slabs - 1)
            def _():
                across_arrived(2, vol.at[:, 5, :, 1 - core]).wait()

        multiply(pair(i, 0), first=i == len(COUPLES), last=i == OWN - 1)
    for c in range(len(COUPLES)):
        tap_arrived3(c).wait()
        multiply(COUPLES[c][0])
        multiply(COUPLES[c][1], last=c == len(COUPLES) - 1)

    def drain_out(i, carry):
        z = i // CHIPS
        k = i % CHIPS

        @pl.when(k == 0)
        def _():
            out_own(z).wait()

        @pl.when(k > 0)
        def _():
            out_copy(z, k).wait_send()
            out_arrived(z, k).wait()

        return carry

    lax.fori_loop(0, PLANES * CHIPS, drain_out, 0)

    def drain_feat(k, carry):
        feat_copy(k).wait_send()
        return carry

    lax.fori_loop(1, CHIPS, drain_feat, 0)
    for i in range(OWN):
        for k in range(1, SIDE):
            tap_copy1(i, k).wait_send()
            tap_copy2(i, k).wait_send()
    for c in range(len(COUPLES)):
        tap_copy3(c).wait_send()
    middle.wait_send()

    @pl.when(slab > 0)
    def _():
        down.wait_send()
        low.wait_send()

    @pl.when(slab < slabs - 1)
    def _():
        up.wait_send()
        high.wait_send()


def body(features, weights, bias_vector):
    DMA = pltpu.SemaphoreType.DMA
    hbm = pl.BlockSpec(memory_space=pltpu.HBM)
    anywhere = pl.BlockSpec(memory_space=pl.ANY)
    flat = weights.reshape(9, 3, 8, 256)
    got = pl.pallas_call(
        kernel,
        out_shape=jax.ShapeDtypeStruct((PLANES, 64, 8, 128), jnp.bfloat16),
        in_specs=[hbm, hbm, hbm],
        out_specs=anywhere,
        scratch_shapes=[
            pltpu.VMEM((PLANES, 8, 64, 128), jnp.bfloat16),
            pltpu.VMEM((256,), jnp.float32),
            pltpu.VMEM((66, PLANES, 8, 128), jnp.bfloat16),
            pltpu.VMEM((ROWS + 2, PLANES + 2, CHIPS, 2, 8, 128), jnp.bfloat16),
            pltpu.VMEM((9, 3, SIDE, SIDE, 8, 256), jnp.bfloat16),
            pltpu.VMEM((PLANES, 384, ROWS * 128), jnp.float32),
            pltpu.VMEM((PLANES, CHIPS, ROWS, 8, 128), jnp.bfloat16),
            pltpu.VMEM((CHIPS, 2, 8, 128), jnp.float32),
            DMA((CHIPS,)), DMA((CHIPS,)),
            DMA((3,)), DMA((3,)),
            DMA((2,)), DMA((2,)),
            DMA((OWN, SIDE)), DMA((OWN, SIDE)),
            DMA((OWN, SIDE)), DMA((OWN, SIDE)),
            DMA((1,)), DMA((1,)),
            DMA((PLANES, CHIPS)), DMA((PLANES, CHIPS)),
            DMA((3 + OWN,)),
        ],
        compiler_params=pltpu.CompilerParams(
            collective_id=0, has_side_effects=True, vmem_limit_bytes=40 * 1024 * 1024
        ),
    )(*[pltpu.with_memory_space_constraint(a, pltpu.HBM) for a in (features, flat, bias_vector)])
    return got.transpose(0, 2, 1, 3)


def solution(mesh):
    placed = (P("slab", "filt", None, None), P(None, None, None, "filt", None), P())
    return jax.shard_map(
        body, mesh=mesh, in_specs=placed, out_specs=P("slab", "filt", None, None), check_vma=False
    )
```

```python
import jax
import jax.numpy as jnp
from jax import lax
from jax.experimental import pallas as pl
from jax.experimental.pallas import tpu as pltpu
from jax.sharding import PartitionSpec as P

MESH = pl.DeviceIdType.MESH
SIDE = 4
CHIPS = 16
ROWS = 4
PLANES = 4
COUPLES = ((0, 6), (2, 8))
COMMON = (3, 4, 5, 1, 7)
OWN = len(COUPLES) + len(COMMON)
X_FIRST = (0, 2, 4, 6)
PARTS = (0, 3, slice(1, 3))
PLACES = (1, 4, slice(2, 4))


def kernel(feat_hbm, w, bias_hbm, out, feat, bias, turned, vol, taps, acc, ready, column,
           f_s, f_r, x_s, x_r, h_s, h_r, w1_s, w1_r, w2_s, w2_r, z_s, z_r, o_s, o_r, l_s):
    slab = lax.axis_index("slab")
    filt = lax.axis_index("filt")
    slabs = lax.axis_size("slab")
    chip = filt // 2
    core = filt % 2
    cy = chip // SIDE
    cx = chip % SIDE

    def device(y, x, c):
        return {"filt": (y * SIDE + x) * 2 + c}

    def partner(k):
        y = (cy + k // SIDE) % SIDE
        x = (cx + k % SIDE) % SIDE
        return y, x

    def source(k):
        y = (cy + SIDE - k // SIDE) % SIDE
        x = (cx + SIDE - k % SIDE) % SIDE
        return y * SIDE + x

    barrier = pltpu.get_barrier_semaphore()

    def greet(k, carry):
        y, x = partner(k)
        pl.semaphore_signal(barrier, inc=1, device_id=device(y, x, core), device_id_type=MESH)
        return carry

    lax.fori_loop(1, CHIPS, greet, 0)
    pl.semaphore_signal(barrier, inc=1, device_id=device(cy, cx, 1 - core), device_id_type=MESH)

    for step in (1, slabs - 1):
        pl.semaphore_signal(
            barrier, inc=1, device_id={"slab": (slab + step) % slabs}, device_id_type=MESH
        )

    odd = slab % 2

    def pair(i, parity):
        if i >= len(COUPLES):
            return COMMON[i - len(COUPLES)]
        first, second = COUPLES[i]
        return first + parity * (second - first)

    take_feat = pltpu.make_async_copy(feat_hbm, feat, l_s.at[0])
    take_feat.start()
    take_bias = pltpu.make_async_copy(bias_hbm, bias, l_s.at[1])
    take_bias.start()
    own_taps = []
    for i in range(OWN):
        unit = pair(i, odd)
        own_taps.append(pltpu.make_async_copy(w.at[unit], taps.at[unit, :, cy, cx], l_s.at[3 + i]))
        own_taps[i].start()

    @pl.when(slab == 0)
    def _():
        for y in range(ROWS + 2):
            vol[y, 0] = jnp.zeros(vol.shape[2:], vol.dtype)

    @pl.when(slab == slabs - 1)
    def _():
        for y in range(ROWS + 2):
            vol[y, 5] = jnp.zeros(vol.shape[2:], vol.dtype)

    turned[0] = jnp.zeros(turned.shape[1:], turned.dtype)
    turned[turned.shape[0] - 1] = jnp.zeros(turned.shape[1:], turned.dtype)
    take_feat.wait()
    for z in range(PLANES):
        turned[1:65, z] = jnp.transpose(feat[z].astype(jnp.float32), (1, 0, 2)).astype(jnp.bfloat16)

    own_feat = pltpu.make_async_copy(
        turned.at[pl.ds(chip * ROWS, ROWS + 2)], vol.at[:, 1:5, chip, core], l_s.at[2]
    )
    own_feat.start()

    take_bias.wait()
    wide = jnp.broadcast_to(bias[...].reshape(1, 256), (128, 256))
    column[...] = jnp.transpose(wide, (1, 0)).reshape(CHIPS, 2, 8, 128)

    pl.semaphore_wait(barrier, CHIPS + 2)

    def feat_copy(g, k):
        y, x = partner(k)
        return pltpu.make_async_remote_copy(
            src_ref=turned.at[pl.ds((y * SIDE + x) * ROWS, ROWS + 2), PARTS[g]],
            dst_ref=vol.at[:, PLACES[g], chip, core],
            send_sem=f_s.at[g, k], recv_sem=f_r.at[g, k],
            device_id=device(y, x, core), device_id_type=MESH,
        )

    def send_feat(g):
        def send(k, carry):
            feat_copy(g, k).start()
            return carry

        lax.fori_loop(1, CHIPS, send, 0)

    def wait_feat(g):
        def wait(k, carry):
            piece = vol.at[:, PLACES[g], source(k), core]
            pltpu.make_async_copy(piece, piece, f_r.at[g, k]).wait()
            return carry

        lax.fori_loop(1, CHIPS, wait, 0)

    def ring(i, k, phase, sign):
        step = k if sign > 0 else SIDE - k
        if (i in X_FIRST) == (phase == 1):
            return cy, (cx + step) % SIDE
        return (cy + step) % SIDE, cx

    def tap_copy1(i, k):
        y, x = ring(i, k, 1, 1)
        return pltpu.make_async_remote_copy(
            src_ref=w.at[pair(i, odd)], dst_ref=taps.at[pair(i, odd), :, cy, cx],
            send_sem=w1_s.at[i, k], recv_sem=w1_r.at[i, k],
            device_id=device(y, x, core), device_id_type=MESH,
        )

    def tap_arrived1(i, k):
        y, x = ring(i, k, 1, -1)
        piece = taps.at[pair(i, odd), :, y, x]
        return pltpu.make_async_copy(piece, piece, w1_r.at[i, k])

    def tap_line(i, y, x):
        if i in X_FIRST:
            return taps.at[pair(i, odd), :, y]
        return taps.at[pair(i, odd), :, :, x]

    def tap_copy2(i, k):
        y, x = ring(i, k, 2, 1)
        line = tap_line(i, cy, cx)
        return pltpu.make_async_remote_copy(
            src_ref=line, dst_ref=line, send_sem=w2_s.at[i, k], recv_sem=w2_r.at[i, k],
            device_id=device(y, x, core), device_id_type=MESH,
        )

    def tap_arrived2(i, k):
        y, x = ring(i, k, 2, -1)
        line = tap_line(i, y, x)
        return pltpu.make_async_copy(line, line, w2_r.at[i, k])

    def tap_copy3(c):
        unit = taps.at[pair(c, odd)]
        step = 1 if c == 0 else slabs - 1
        return pltpu.make_async_remote_copy(
            src_ref=unit, dst_ref=unit, send_sem=z_s.at[c], recv_sem=z_r.at[c],
            device_id={"slab": (slab + step) % slabs}, device_id_type=MESH,
        )

    def tap_arrived3(c):
        unit = taps.at[pair(c, 1 - odd)]
        return pltpu.make_async_copy(unit, unit, z_r.at[c])

    def second_phase(which):
        for i in which:
            own_taps[i].wait()
            for k in range(1, SIDE):
                tap_arrived1(i, k).wait()
            for k in range(1, SIDE):
                tap_copy2(i, k).start()

    def third_phase():
        for c in range(len(COUPLES)):
            for k in range(1, SIDE):
                tap_arrived2(c, k).wait()
            tap_copy3(c).start()

    def across(index, part):
        return pltpu.make_async_remote_copy(
            src_ref=part, dst_ref=part, send_sem=x_s.at[index], recv_sem=x_r.at[index],
            device_id=device(cy, cx, 1 - core), device_id_type=MESH,
        )

    def across_arrived(index, part):
        return pltpu.make_async_copy(part, part, x_r.at[index])

    down = pltpu.make_async_remote_copy(
        src_ref=vol.at[:, 1, :, core], dst_ref=vol.at[:, 5, :, core],
        send_sem=h_s.at[0], recv_sem=h_r.at[0],
        device_id={"slab": slab - 1}, device_id_type=MESH,
    )
    up = pltpu.make_async_remote_copy(
        src_ref=vol.at[:, 4, :, core], dst_ref=vol.at[:, 0, :, core],
        send_sem=h_s.at[1], recv_sem=h_r.at[1],
        device_id={"slab": slab + 1}, device_id_type=MESH,
    )

    send_feat(0)
    send_feat(1)
    for i in range(OWN):
        for k in range(1, SIDE):
            tap_copy1(i, k).start()
    send_feat(2)
    own_feat.wait()
    wait_feat(0)

    @pl.when(slab > 0)
    def _():
        down.start()

    bottom = across(0, vol.at[:, 1, :, core])
    bottom.start()
    wait_feat(1)

    @pl.when(slab < slabs - 1)
    def _():
        up.start()

    top = across(3, vol.at[:, 4, :, core])
    top.start()
    second_phase(range(len(COUPLES)))
    second_phase(range(len(COUPLES), OWN))
    wait_feat(2)
    middle = across(4, vol.at[:, 2:4, :, core])
    middle.start()
    third_phase()

    low = across(1, vol.at[:, 0, :, core])
    high = across(2, vol.at[:, 5, :, core])
    across_arrived(0, vol.at[:, 1, :, 1 - core]).wait()
    across_arrived(3, vol.at[:, 4, :, 1 - core]).wait()
    across_arrived(4, vol.at[:, 2:4, :, 1 - core]).wait()

    lane = lax.broadcasted_iota(jnp.int32, (128, 128), 1)

    def out_copy(z, k):
        y, x = partner(k)
        return pltpu.make_async_remote_copy(
            src_ref=ready.at[z, y * SIDE + x], dst_ref=out.at[z, pl.ds(chip * ROWS, ROWS)],
            send_sem=o_s.at[z, k], recv_sem=o_r.at[z, k],
            device_id=device(y, x, core), device_id_type=MESH,
        )

    def out_arrived(z, k):
        piece = out.at[z, pl.ds(source(k) * ROWS, ROWS)]
        return pltpu.make_async_copy(piece, piece, o_r.at[z, k])

    def out_own(z):
        return pltpu.make_async_copy(
            ready.at[z, chip], out.at[z, pl.ds(chip * ROWS, ROWS)], o_s.at[z, 0]
        )

    def finish(z):
        biases = column[:, core].reshape(128, 128)
        for y in range(ROWS):
            part = acc[z, :, y * 128 : (y + 1) * 128]
            before = jnp.where(lane == 0, 0.0, pltpu.roll(part[0:128], 1, 1))
            after = jnp.where(lane == 127, 0.0, pltpu.roll(part[256:384], 127, 1))
            shifted = before + part[128:256] + after + biases
            active = jnp.where(shifted > 0, shifted, 0.3 * shifted)
            ready[z, :, y] = active.reshape(CHIPS, 8, 128).astype(jnp.bfloat16)
        out_own(z).start()

        def send(k, carry):
            out_copy(z, k).start()
            return carry

        lax.fori_loop(1, CHIPS, send, 0)

    def multiply(unit, first=False, last=False):
        dz, dy = unit // 3, unit % 3
        lines = [
            vol[dy + y, z + dz].reshape(256, 128) for z in range(PLANES) for y in range(ROWS)
        ]
        product = jnp.dot(
            taps[unit].reshape(384, 256),
            jnp.concatenate(lines, axis=1),
            preferred_element_type=jnp.float32,
        )
        for z in range(PLANES):
            part = product[:, z * ROWS * 128 : (z + 1) * ROWS * 128]
            if first:
                acc[z] = part
            else:
                acc[z] += part
            if last:
                finish(z)

    for i in range(len(COUPLES), OWN):
        for k in range(1, SIDE):
            tap_arrived2(i, k).wait()
        if i == len(COUPLES) + 1:
            @pl.when(slab > 0)
            def _():
                edge = vol.at[:, 0, :, core]
                pltpu.make_async_copy(edge, edge, h_r.at[1]).wait()
                low.start()

            @pl.when(slab < slabs - 1)
            def _():
                edge = vol.at[:, 5, :, core]
                pltpu.make_async_copy(edge, edge, h_r.at[0]).wait()
                high.start()

        if i == len(COUPLES) + 3:
            @pl.when(slab > 0)
            def _():
                across_arrived(1, vol.at[:, 0, :, 1 - core]).wait()

            @pl.when(slab < slabs - 1)
            def _():
                across_arrived(2, vol.at[:, 5, :, 1 - core]).wait()

        if i == OWN - 1:
            for c in range(len(COUPLES)):
                tap_arrived3(c).wait()
                multiply(COUPLES[c][0])
                multiply(COUPLES[c][1])
        multiply(pair(i, 0), first=i == len(COUPLES), last=i == OWN - 1)

    def drain_out(i, carry):
        z = i // CHIPS
        k = i % CHIPS

        @pl.when(k == 0)
        def _():
            out_own(z).wait()

        @pl.when(k > 0)
        def _():
            out_copy(z, k).wait_send()
            out_arrived(z, k).wait()

        return carry

    lax.fori_loop(0, PLANES * CHIPS, drain_out, 0)

    def drain_feat(k, carry):
        for g in range(len(PARTS)):
            feat_copy(g, k).wait_send()
        return carry

    lax.fori_loop(1, CHIPS, drain_feat, 0)
    for i in range(OWN):
        for k in range(1, SIDE):
            tap_copy1(i, k).wait_send()
            tap_copy2(i, k).wait_send()
    for c in range(len(COUPLES)):
        tap_copy3(c).wait_send()
    bottom.wait_send()
    top.wait_send()
    middle.wait_send()

    @pl.when(slab > 0)
    def _():
        down.wait_send()
        low.wait_send()

    @pl.when(slab < slabs - 1)
    def _():
        up.wait_send()
        high.wait_send()


def body(features, weights, bias_vector):
    DMA = pltpu.SemaphoreType.DMA
    hbm = pl.BlockSpec(memory_space=pltpu.HBM)
    anywhere = pl.BlockSpec(memory_space=pl.ANY)
    flat = weights.reshape(9, 3, 8, 256)
    got = pl.pallas_call(
        kernel,
        out_shape=jax.ShapeDtypeStruct((PLANES, 64, 8, 128), jnp.bfloat16),
        in_specs=[hbm, hbm, hbm],
        out_specs=anywhere,
        scratch_shapes=[
            pltpu.VMEM((PLANES, 8, 64, 128), jnp.bfloat16),
            pltpu.VMEM((256,), jnp.float32),
            pltpu.VMEM((66, PLANES, 8, 128), jnp.bfloat16),
            pltpu.VMEM((ROWS + 2, PLANES + 2, CHIPS, 2, 8, 128), jnp.bfloat16),
            pltpu.VMEM((9, 3, SIDE, SIDE, 8, 256), jnp.bfloat16),
            pltpu.VMEM((PLANES, 384, ROWS * 128), jnp.float32),
            pltpu.VMEM((PLANES, CHIPS, ROWS, 8, 128), jnp.bfloat16),
            pltpu.VMEM((CHIPS, 2, 8, 128), jnp.float32),
            DMA((len(PARTS), CHIPS)), DMA((len(PARTS), CHIPS)),
            DMA((5,)), DMA((5,)),
            DMA((2,)), DMA((2,)),
            DMA((OWN, SIDE)), DMA((OWN, SIDE)),
            DMA((OWN, SIDE)), DMA((OWN, SIDE)),
            DMA((len(COUPLES),)), DMA((len(COUPLES),)),
            DMA((PLANES, CHIPS)), DMA((PLANES, CHIPS)),
            DMA((3 + OWN,)),
        ],
        compiler_params=pltpu.CompilerParams(
            collective_id=0, has_side_effects=True, vmem_limit_bytes=40 * 1024 * 1024
        ),
    )(*[pltpu.with_memory_space_constraint(a, pltpu.HBM) for a in (features, flat, bias_vector)])
    return got.transpose(0, 2, 1, 3)


def solution(mesh):
    placed = (P("slab", "filt", None, None), P(None, None, None, "filt", None), P())
    return jax.shard_map(
        body, mesh=mesh, in_specs=placed, out_specs=P("slab", "filt", None, None), check_vma=False
    )
```

```python
import jax
import jax.numpy as jnp
from jax import lax
from jax.experimental import pallas as pl
from jax.experimental.pallas import tpu as pltpu
from jax.sharding import PartitionSpec as P

MESH = pl.DeviceIdType.MESH
SIDE = 4
CHIPS = 16
ROWS = 4
PLANES = 4
COUPLES = ((0, 6), (2, 8))
COMMON = (3, 4, 5, 1, 7)
OWN = len(COUPLES) + len(COMMON)
X_FIRST = (0, 2, 4, 6)
PARTS = (0, 3, slice(1, 3))
PLACES = (1, 4, slice(2, 4))
FAR = (10, 6, 9, 14, 11, 2, 8, 5, 15, 7, 13, 1, 4, 3, 12)


def kernel(feat_hbm, w, bias_hbm, out, feat, bias, turned, vol, taps, acc, ready, column,
           f_s, f_r, x_s, x_r, h_s, h_r, w1_s, w1_r, w2_s, w2_r, z_s, z_r, o_s, o_r, l_s):
    slab = lax.axis_index("slab")
    filt = lax.axis_index("filt")
    slabs = lax.axis_size("slab")
    chip = filt // 2
    core = filt % 2
    cy = chip // SIDE
    cx = chip % SIDE

    def device(y, x, c):
        return {"filt": (y * SIDE + x) * 2 + c}

    def partner(k):
        y = (cy + k // SIDE) % SIDE
        x = (cx + k % SIDE) % SIDE
        return y, x

    def source(k):
        y = (cy + SIDE - k // SIDE) % SIDE
        x = (cx + SIDE - k % SIDE) % SIDE
        return y * SIDE + x

    barrier = pltpu.get_barrier_semaphore()

    def greet(k, carry):
        y, x = partner(k)
        pl.semaphore_signal(barrier, inc=1, device_id=device(y, x, core), device_id_type=MESH)
        return carry

    lax.fori_loop(1, CHIPS, greet, 0)
    pl.semaphore_signal(barrier, inc=1, device_id=device(cy, cx, 1 - core), device_id_type=MESH)

    for step in (1, slabs - 1):
        pl.semaphore_signal(
            barrier, inc=1, device_id={"slab": (slab + step) % slabs}, device_id_type=MESH
        )

    odd = slab % 2

    def pair(i, parity):
        if i >= len(COUPLES):
            return COMMON[i - len(COUPLES)]
        first, second = COUPLES[i]
        return first + parity * (second - first)

    take_feat = pltpu.make_async_copy(feat_hbm, feat, l_s.at[0])
    take_feat.start()
    take_bias = pltpu.make_async_copy(bias_hbm, bias, l_s.at[1])
    take_bias.start()
    own_taps = []
    for i in range(OWN):
        unit = pair(i, odd)
        own_taps.append(pltpu.make_async_copy(w.at[unit], taps.at[unit, :, cy, cx], l_s.at[3 + i]))
        own_taps[i].start()

    @pl.when(slab == 0)
    def _():
        for y in range(ROWS + 2):
            vol[y, 0] = jnp.zeros(vol.shape[2:], vol.dtype)

    @pl.when(slab == slabs - 1)
    def _():
        for y in range(ROWS + 2):
            vol[y, 5] = jnp.zeros(vol.shape[2:], vol.dtype)

    turned[0] = jnp.zeros(turned.shape[1:], turned.dtype)
    turned[turned.shape[0] - 1] = jnp.zeros(turned.shape[1:], turned.dtype)
    take_feat.wait()
    for z in range(PLANES):
        turned[1:65, z] = jnp.transpose(feat[z].astype(jnp.float32), (1, 0, 2)).astype(jnp.bfloat16)

    own_feat = pltpu.make_async_copy(
        turned.at[pl.ds(chip * ROWS, ROWS + 2)], vol.at[:, 1:5, chip, core], l_s.at[2]
    )
    own_feat.start()

    take_bias.wait()
    wide = jnp.broadcast_to(bias[...].reshape(1, 256), (128, 256))
    column[...] = jnp.transpose(wide, (1, 0)).reshape(CHIPS, 2, 8, 128)

    pl.semaphore_wait(barrier, CHIPS + 2)

    def feat_copy(g, k):
        y, x = partner(k)
        return pltpu.make_async_remote_copy(
            src_ref=turned.at[pl.ds((y * SIDE + x) * ROWS, ROWS + 2), PARTS[g]],
            dst_ref=vol.at[:, PLACES[g], chip, core],
            send_sem=f_s.at[g, k], recv_sem=f_r.at[g, k],
            device_id=device(y, x, core), device_id_type=MESH,
        )

    def send_feat(g):
        for k in FAR:
            feat_copy(g, k).start()

    def wait_feat(g):
        def wait(k, carry):
            piece = vol.at[:, PLACES[g], source(k), core]
            pltpu.make_async_copy(piece, piece, f_r.at[g, k]).wait()
            return carry

        lax.fori_loop(1, CHIPS, wait, 0)

    def ring(i, k, phase, sign):
        step = k if sign > 0 else SIDE - k
        if (i in X_FIRST) == (phase == 1):
            return cy, (cx + step) % SIDE
        return (cy + step) % SIDE, cx

    def tap_copy1(i, k):
        y, x = ring(i, k, 1, 1)
        return pltpu.make_async_remote_copy(
            src_ref=w.at[pair(i, odd)], dst_ref=taps.at[pair(i, odd), :, cy, cx],
            send_sem=w1_s.at[i, k], recv_sem=w1_r.at[i, k],
            device_id=device(y, x, core), device_id_type=MESH,
        )

    def tap_arrived1(i, k):
        y, x = ring(i, k, 1, -1)
        piece = taps.at[pair(i, odd), :, y, x]
        return pltpu.make_async_copy(piece, piece, w1_r.at[i, k])

    def tap_line(i, y, x):
        if i in X_FIRST:
            return taps.at[pair(i, odd), :, y]
        return taps.at[pair(i, odd), :, :, x]

    def tap_copy2(i, k):
        y, x = ring(i, k, 2, 1)
        line = tap_line(i, cy, cx)
        return pltpu.make_async_remote_copy(
            src_ref=line, dst_ref=line, send_sem=w2_s.at[i, k], recv_sem=w2_r.at[i, k],
            device_id=device(y, x, core), device_id_type=MESH,
        )

    def tap_arrived2(i, k):
        y, x = ring(i, k, 2, -1)
        line = tap_line(i, y, x)
        return pltpu.make_async_copy(line, line, w2_r.at[i, k])

    def tap_copy3(c):
        unit = taps.at[pair(c, odd)]
        step = 1 if c == 0 else slabs - 1
        return pltpu.make_async_remote_copy(
            src_ref=unit, dst_ref=unit, send_sem=z_s.at[c], recv_sem=z_r.at[c],
            device_id={"slab": (slab + step) % slabs}, device_id_type=MESH,
        )

    def tap_arrived3(c):
        unit = taps.at[pair(c, 1 - odd)]
        return pltpu.make_async_copy(unit, unit, z_r.at[c])

    def second_phase(which):
        for i in which:
            own_taps[i].wait()
            for k in range(1, SIDE):
                tap_arrived1(i, k).wait()
            for k in (2, 1, 3):
                tap_copy2(i, k).start()

    def third_phase():
        for c in range(len(COUPLES)):
            for k in range(1, SIDE):
                tap_arrived2(c, k).wait()
            tap_copy3(c).start()

    def across(index, part):
        return pltpu.make_async_remote_copy(
            src_ref=part, dst_ref=part, send_sem=x_s.at[index], recv_sem=x_r.at[index],
            device_id=device(cy, cx, 1 - core), device_id_type=MESH,
        )

    def across_arrived(index, part):
        return pltpu.make_async_copy(part, part, x_r.at[index])

    down = pltpu.make_async_remote_copy(
        src_ref=vol.at[:, 1, :, core], dst_ref=vol.at[:, 5, :, core],
        send_sem=h_s.at[0], recv_sem=h_r.at[0],
        device_id={"slab": slab - 1}, device_id_type=MESH,
    )
    up = pltpu.make_async_remote_copy(
        src_ref=vol.at[:, 4, :, core], dst_ref=vol.at[:, 0, :, core],
        send_sem=h_s.at[1], recv_sem=h_r.at[1],
        device_id={"slab": slab + 1}, device_id_type=MESH,
    )

    send_feat(0)
    send_feat(1)
    for i in range(OWN):
        for k in range(1, SIDE):
            tap_copy1(i, k).start()
    send_feat(2)
    own_feat.wait()
    wait_feat(0)

    @pl.when(slab > 0)
    def _():
        down.start()

    bottom = across(0, vol.at[:, 1, :, core])
    bottom.start()
    wait_feat(1)

    @pl.when(slab < slabs - 1)
    def _():
        up.start()

    top = across(3, vol.at[:, 4, :, core])
    top.start()
    second_phase(range(len(COUPLES)))
    second_phase(range(len(COUPLES), OWN))
    wait_feat(2)
    middle = across(4, vol.at[:, 2:4, :, core])
    middle.start()
    third_phase()

    low = across(1, vol.at[:, 0, :, core])
    high = across(2, vol.at[:, 5, :, core])
    across_arrived(0, vol.at[:, 1, :, 1 - core]).wait()
    across_arrived(3, vol.at[:, 4, :, 1 - core]).wait()
    across_arrived(4, vol.at[:, 2:4, :, 1 - core]).wait()

    lane = lax.broadcasted_iota(jnp.int32, (128, 128), 1)

    def out_copy(z, k):
        y, x = partner(k)
        return pltpu.make_async_remote_copy(
            src_ref=ready.at[z, y * SIDE + x], dst_ref=out.at[z, pl.ds(chip * ROWS, ROWS)],
            send_sem=o_s.at[z, k], recv_sem=o_r.at[z, k],
            device_id=device(y, x, core), device_id_type=MESH,
        )

    def out_arrived(z, k):
        piece = out.at[z, pl.ds(source(k) * ROWS, ROWS)]
        return pltpu.make_async_copy(piece, piece, o_r.at[z, k])

    def out_own(z):
        return pltpu.make_async_copy(
            ready.at[z, chip], out.at[z, pl.ds(chip * ROWS, ROWS)], o_s.at[z, 0]
        )

    def finish(z):
        biases = column[:, core].reshape(128, 128)
        for y in range(ROWS):
            part = acc[z, :, y * 128 : (y + 1) * 128]
            before = jnp.where(lane == 0, 0.0, pltpu.roll(part[0:128], 1, 1))
            after = jnp.where(lane == 127, 0.0, pltpu.roll(part[256:384], 127, 1))
            shifted = before + part[128:256] + after + biases
            active = jnp.where(shifted > 0, shifted, 0.3 * shifted)
            ready[z, :, y] = active.reshape(CHIPS, 8, 128).astype(jnp.bfloat16)
        out_own(z).start()

        for k in FAR:
            out_copy(z, k).start()

    def multiply(unit, first=False, last=False):
        dz, dy = unit // 3, unit % 3
        lines = [
            vol[dy + y, z + dz].reshape(256, 128) for z in range(PLANES) for y in range(ROWS)
        ]
        product = jnp.dot(
            taps[unit].reshape(384, 256),
            jnp.concatenate(lines, axis=1),
            preferred_element_type=jnp.float32,
        )
        for z in range(PLANES):
            part = product[:, z * ROWS * 128 : (z + 1) * ROWS * 128]
            if first:
                acc[z] = part
            else:
                acc[z] += part
            if last:
                finish(z)

    for i in range(len(COUPLES), OWN):
        for k in range(1, SIDE):
            tap_arrived2(i, k).wait()
        if i == len(COUPLES) + 1:
            @pl.when(slab > 0)
            def _():
                edge = vol.at[:, 0, :, core]
                pltpu.make_async_copy(edge, edge, h_r.at[1]).wait()
                low.start()

            @pl.when(slab < slabs - 1)
            def _():
                edge = vol.at[:, 5, :, core]
                pltpu.make_async_copy(edge, edge, h_r.at[0]).wait()
                high.start()

        if i == len(COUPLES) + 3:
            @pl.when(slab > 0)
            def _():
                across_arrived(1, vol.at[:, 0, :, 1 - core]).wait()

            @pl.when(slab < slabs - 1)
            def _():
                across_arrived(2, vol.at[:, 5, :, 1 - core]).wait()

        if i == OWN - 1:
            for c in range(len(COUPLES)):
                tap_arrived3(c).wait()
                multiply(COUPLES[c][0])
                multiply(COUPLES[c][1])
        multiply(pair(i, 0), first=i == len(COUPLES), last=i == OWN - 1)

    def drain_out(i, carry):
        z = i // CHIPS
        k = i % CHIPS

        @pl.when(k == 0)
        def _():
            out_own(z).wait()

        @pl.when(k > 0)
        def _():
            out_copy(z, k).wait_send()
            out_arrived(z, k).wait()

        return carry

    lax.fori_loop(0, PLANES * CHIPS, drain_out, 0)

    def drain_feat(k, carry):
        for g in range(len(PARTS)):
            feat_copy(g, k).wait_send()
        return carry

    lax.fori_loop(1, CHIPS, drain_feat, 0)
    for i in range(OWN):
        for k in range(1, SIDE):
            tap_copy1(i, k).wait_send()
            tap_copy2(i, k).wait_send()
    for c in range(len(COUPLES)):
        tap_copy3(c).wait_send()
    bottom.wait_send()
    top.wait_send()
    middle.wait_send()

    @pl.when(slab > 0)
    def _():
        down.wait_send()
        low.wait_send()

    @pl.when(slab < slabs - 1)
    def _():
        up.wait_send()
        high.wait_send()


def body(features, weights, bias_vector):
    DMA = pltpu.SemaphoreType.DMA
    hbm = pl.BlockSpec(memory_space=pltpu.HBM)
    anywhere = pl.BlockSpec(memory_space=pl.ANY)
    flat = weights.reshape(9, 3, 8, 256)
    got = pl.pallas_call(
        kernel,
        out_shape=jax.ShapeDtypeStruct((PLANES, 64, 8, 128), jnp.bfloat16),
        in_specs=[hbm, hbm, hbm],
        out_specs=anywhere,
        scratch_shapes=[
            pltpu.VMEM((PLANES, 8, 64, 128), jnp.bfloat16),
            pltpu.VMEM((256,), jnp.float32),
            pltpu.VMEM((66, PLANES, 8, 128), jnp.bfloat16),
            pltpu.VMEM((ROWS + 2, PLANES + 2, CHIPS, 2, 8, 128), jnp.bfloat16),
            pltpu.VMEM((9, 3, SIDE, SIDE, 8, 256), jnp.bfloat16),
            pltpu.VMEM((PLANES, 384, ROWS * 128), jnp.float32),
            pltpu.VMEM((PLANES, CHIPS, ROWS, 8, 128), jnp.bfloat16),
            pltpu.VMEM((CHIPS, 2, 8, 128), jnp.float32),
            DMA((len(PARTS), CHIPS)), DMA((len(PARTS), CHIPS)),
            DMA((5,)), DMA((5,)),
            DMA((2,)), DMA((2,)),
            DMA((OWN, SIDE)), DMA((OWN, SIDE)),
            DMA((OWN, SIDE)), DMA((OWN, SIDE)),
            DMA((len(COUPLES),)), DMA((len(COUPLES),)),
            DMA((PLANES, CHIPS)), DMA((PLANES, CHIPS)),
            DMA((3 + OWN,)),
        ],
        compiler_params=pltpu.CompilerParams(
            collective_id=0, has_side_effects=True, vmem_limit_bytes=40 * 1024 * 1024
        ),
    )(*[pltpu.with_memory_space_constraint(a, pltpu.HBM) for a in (features, flat, bias_vector)])
    return got.transpose(0, 2, 1, 3)


def solution(mesh):
    placed = (P("slab", "filt", None, None), P(None, None, None, "filt", None), P())
    return jax.shard_map(
        body, mesh=mesh, in_specs=placed, out_specs=P("slab", "filt", None, None), check_vma=False
    )
```

```python
import jax
import jax.numpy as jnp
from jax import lax
from jax.experimental import pallas as pl
from jax.experimental.pallas import tpu as pltpu
from jax.sharding import PartitionSpec as P

MESH = pl.DeviceIdType.MESH
SIDE = 4
CHIPS = 16
ROWS = 4
PLANES = 4
COUPLES = ((0, 6), (2, 8))
COMMON = (3, 4, 5, 1, 7)
OWN = len(COUPLES) + len(COMMON)
X_FIRST = (1, 3, 5)
PARTS = (0, 3, slice(1, 3))
PLACES = (1, 4, slice(2, 4))
FAR = (10, 6, 9, 14, 11, 2, 8, 5, 15, 7, 13, 1, 4, 3, 12)


def kernel(feat_hbm, w, bias_hbm, out, feat, bias, turned, vol, taps, acc, ready, column,
           f_s, f_r, x_s, x_r, h_s, h_r, w1_s, w1_r, w2_s, w2_r, z_s, z_r, o_s, o_r, l_s):
    slab = lax.axis_index("slab")
    filt = lax.axis_index("filt")
    slabs = lax.axis_size("slab")
    chip = filt // 2
    core = filt % 2
    cy = chip // SIDE
    cx = chip % SIDE

    def device(y, x, c):
        return {"filt": (y * SIDE + x) * 2 + c}

    def partner(k):
        y = (cy + k // SIDE) % SIDE
        x = (cx + k % SIDE) % SIDE
        return y, x

    def source(k):
        y = (cy + SIDE - k // SIDE) % SIDE
        x = (cx + SIDE - k % SIDE) % SIDE
        return y * SIDE + x

    barrier = pltpu.get_barrier_semaphore()

    def greet(k, carry):
        y, x = partner(k)
        pl.semaphore_signal(barrier, inc=1, device_id=device(y, x, core), device_id_type=MESH)
        return carry

    lax.fori_loop(1, CHIPS, greet, 0)
    pl.semaphore_signal(barrier, inc=1, device_id=device(cy, cx, 1 - core), device_id_type=MESH)

    for step in (1, slabs - 1):
        pl.semaphore_signal(
            barrier, inc=1, device_id={"slab": (slab + step) % slabs}, device_id_type=MESH
        )

    odd = slab % 2

    def pair(i, parity):
        if i >= len(COUPLES):
            return COMMON[i - len(COUPLES)]
        first, second = COUPLES[i]
        return first + parity * (second - first)

    take_feat = pltpu.make_async_copy(feat_hbm, feat, l_s.at[0])
    take_feat.start()
    take_bias = pltpu.make_async_copy(bias_hbm, bias, l_s.at[1])
    take_bias.start()
    own_taps = []
    for i in range(OWN):
        unit = pair(i, odd)
        own_taps.append(pltpu.make_async_copy(w.at[unit], taps.at[unit, :, cy, cx], l_s.at[3 + i]))
        own_taps[i].start()

    @pl.when(slab == 0)
    def _():
        for y in range(ROWS + 2):
            vol[y, 0] = jnp.zeros(vol.shape[2:], vol.dtype)

    @pl.when(slab == slabs - 1)
    def _():
        for y in range(ROWS + 2):
            vol[y, 5] = jnp.zeros(vol.shape[2:], vol.dtype)

    turned[0] = jnp.zeros(turned.shape[1:], turned.dtype)
    turned[turned.shape[0] - 1] = jnp.zeros(turned.shape[1:], turned.dtype)
    take_feat.wait()
    for z in range(PLANES):
        turned[1:65, z] = jnp.transpose(feat[z].astype(jnp.float32), (1, 0, 2)).astype(jnp.bfloat16)

    own_feat = pltpu.make_async_copy(
        turned.at[pl.ds(chip * ROWS, ROWS + 2)], vol.at[:, 1:5, chip, core], l_s.at[2]
    )
    own_feat.start()

    take_bias.wait()
    wide = jnp.broadcast_to(bias[...].reshape(1, 256), (128, 256))
    column[...] = jnp.transpose(wide, (1, 0)).reshape(CHIPS, 2, 8, 128)

    pl.semaphore_wait(barrier, CHIPS + 2)

    def feat_copy(g, k):
        y, x = partner(k)
        return pltpu.make_async_remote_copy(
            src_ref=turned.at[pl.ds((y * SIDE + x) * ROWS, ROWS + 2), PARTS[g]],
            dst_ref=vol.at[:, PLACES[g], chip, core],
            send_sem=f_s.at[g, k], recv_sem=f_r.at[g, k],
            device_id=device(y, x, core), device_id_type=MESH,
        )

    def send_feat(g):
        for k in FAR:
            feat_copy(g, k).start()

    def wait_feat(g):
        def wait(k, carry):
            piece = vol.at[:, PLACES[g], source(k), core]
            pltpu.make_async_copy(piece, piece, f_r.at[g, k]).wait()
            return carry

        lax.fori_loop(1, CHIPS, wait, 0)

    def ring(i, k, phase, sign):
        step = k if sign > 0 else SIDE - k
        if (i in X_FIRST) == (phase == 1):
            return cy, (cx + step) % SIDE
        return (cy + step) % SIDE, cx

    def tap_copy1(i, k):
        y, x = ring(i, k, 1, 1)
        return pltpu.make_async_remote_copy(
            src_ref=w.at[pair(i, odd)], dst_ref=taps.at[pair(i, odd), :, cy, cx],
            send_sem=w1_s.at[i, k], recv_sem=w1_r.at[i, k],
            device_id=device(y, x, core), device_id_type=MESH,
        )

    def tap_arrived1(i, k):
        y, x = ring(i, k, 1, -1)
        piece = taps.at[pair(i, odd), :, y, x]
        return pltpu.make_async_copy(piece, piece, w1_r.at[i, k])

    def tap_line(i, y, x):
        if i in X_FIRST:
            return taps.at[pair(i, odd), :, y]
        return taps.at[pair(i, odd), :, :, x]

    def tap_copy2(i, k):
        y, x = ring(i, k, 2, 1)
        line = tap_line(i, cy, cx)
        return pltpu.make_async_remote_copy(
            src_ref=line, dst_ref=line, send_sem=w2_s.at[i, k], recv_sem=w2_r.at[i, k],
            device_id=device(y, x, core), device_id_type=MESH,
        )

    def tap_arrived2(i, k):
        y, x = ring(i, k, 2, -1)
        line = tap_line(i, y, x)
        return pltpu.make_async_copy(line, line, w2_r.at[i, k])

    def tap_copy3(c):
        unit = taps.at[pair(c, odd)]
        step = 1 if c == 0 else slabs - 1
        return pltpu.make_async_remote_copy(
            src_ref=unit, dst_ref=unit, send_sem=z_s.at[c], recv_sem=z_r.at[c],
            device_id={"slab": (slab + step) % slabs}, device_id_type=MESH,
        )

    def tap_arrived3(c):
        unit = taps.at[pair(c, 1 - odd)]
        return pltpu.make_async_copy(unit, unit, z_r.at[c])

    def second_phase(which):
        for i in which:
            own_taps[i].wait()
            for k in range(1, SIDE):
                tap_arrived1(i, k).wait()
            for k in (2, 1, 3):
                tap_copy2(i, k).start()

    def third_phase():
        for c in range(len(COUPLES)):
            for k in range(1, SIDE):
                tap_arrived2(c, k).wait()
            tap_copy3(c).start()

    def across(index, part):
        return pltpu.make_async_remote_copy(
            src_ref=part, dst_ref=part, send_sem=x_s.at[index], recv_sem=x_r.at[index],
            device_id=device(cy, cx, 1 - core), device_id_type=MESH,
        )

    def across_arrived(index, part):
        return pltpu.make_async_copy(part, part, x_r.at[index])

    down = pltpu.make_async_remote_copy(
        src_ref=vol.at[:, 1, :, core], dst_ref=vol.at[:, 5, :, core],
        send_sem=h_s.at[0], recv_sem=h_r.at[0],
        device_id={"slab": slab - 1}, device_id_type=MESH,
    )
    up = pltpu.make_async_remote_copy(
        src_ref=vol.at[:, 4, :, core], dst_ref=vol.at[:, 0, :, core],
        send_sem=h_s.at[1], recv_sem=h_r.at[1],
        device_id={"slab": slab + 1}, device_id_type=MESH,
    )

    send_feat(0)
    send_feat(1)
    for i in range(OWN):
        for k in range(1, SIDE):
            tap_copy1(i, k).start()
    send_feat(2)
    own_feat.wait()
    wait_feat(0)

    @pl.when(slab > 0)
    def _():
        down.start()

    bottom = across(0, vol.at[:, 1, :, core])
    bottom.start()
    wait_feat(1)

    @pl.when(slab < slabs - 1)
    def _():
        up.start()

    top = across(3, vol.at[:, 4, :, core])
    top.start()
    second_phase(range(len(COUPLES)))
    second_phase(range(len(COUPLES), OWN))
    wait_feat(2)
    middle = across(4, vol.at[:, 2:4, :, core])
    middle.start()
    third_phase()

    low = across(1, vol.at[:, 0, :, core])
    high = across(2, vol.at[:, 5, :, core])
    across_arrived(0, vol.at[:, 1, :, 1 - core]).wait()
    across_arrived(3, vol.at[:, 4, :, 1 - core]).wait()
    across_arrived(4, vol.at[:, 2:4, :, 1 - core]).wait()

    lane = lax.broadcasted_iota(jnp.int32, (128, 128), 1)

    def out_copy(z, k):
        y, x = partner(k)
        return pltpu.make_async_remote_copy(
            src_ref=ready.at[z, y * SIDE + x], dst_ref=out.at[z, pl.ds(chip * ROWS, ROWS)],
            send_sem=o_s.at[z, k], recv_sem=o_r.at[z, k],
            device_id=device(y, x, core), device_id_type=MESH,
        )

    def out_arrived(z, k):
        piece = out.at[z, pl.ds(source(k) * ROWS, ROWS)]
        return pltpu.make_async_copy(piece, piece, o_r.at[z, k])

    def out_own(z):
        return pltpu.make_async_copy(
            ready.at[z, chip], out.at[z, pl.ds(chip * ROWS, ROWS)], o_s.at[z, 0]
        )

    def finish(z):
        biases = column[:, core].reshape(128, 128)
        for y in range(ROWS):
            part = acc[z, :, y * 128 : (y + 1) * 128]
            before = jnp.where(lane == 0, 0.0, pltpu.roll(part[0:128], 1, 1))
            after = jnp.where(lane == 127, 0.0, pltpu.roll(part[256:384], 127, 1))
            shifted = before + part[128:256] + after + biases
            active = jnp.where(shifted > 0, shifted, 0.3 * shifted)
            ready[z, :, y] = active.reshape(CHIPS, 8, 128).astype(jnp.bfloat16)
        out_own(z).start()

        for k in FAR:
            out_copy(z, k).start()

    def multiply(unit, first=False, last=False):
        dz, dy = unit // 3, unit % 3
        lines = [
            vol[dy + y, z + dz].reshape(256, 128) for z in range(PLANES) for y in range(ROWS)
        ]
        product = jnp.dot(
            taps[unit].reshape(384, 256),
            jnp.concatenate(lines, axis=1),
            preferred_element_type=jnp.float32,
        )
        for z in range(PLANES):
            part = product[:, z * ROWS * 128 : (z + 1) * ROWS * 128]
            if first:
                acc[z] = part
            else:
                acc[z] += part
            if last:
                finish(z)

    for i in range(len(COUPLES), OWN):
        for k in range(1, SIDE):
            tap_arrived2(i, k).wait()
        if i == len(COUPLES) + 1:
            @pl.when(slab > 0)
            def _():
                edge = vol.at[:, 0, :, core]
                pltpu.make_async_copy(edge, edge, h_r.at[1]).wait()
                low.start()

            @pl.when(slab < slabs - 1)
            def _():
                edge = vol.at[:, 5, :, core]
                pltpu.make_async_copy(edge, edge, h_r.at[0]).wait()
                high.start()

        if i == len(COUPLES) + 3:
            @pl.when(slab > 0)
            def _():
                across_arrived(1, vol.at[:, 0, :, 1 - core]).wait()

            @pl.when(slab < slabs - 1)
            def _():
                across_arrived(2, vol.at[:, 5, :, 1 - core]).wait()

        if i == OWN - 1:
            for c in range(len(COUPLES)):
                tap_arrived3(c).wait()
                multiply(COUPLES[c][0])
                multiply(COUPLES[c][1])
        multiply(pair(i, 0), first=i == len(COUPLES), last=i == OWN - 1)

    def drain_out(i, carry):
        z = i // CHIPS
        k = i % CHIPS

        @pl.when(k == 0)
        def _():
            out_own(z).wait()

        @pl.when(k > 0)
        def _():
            out_copy(z, k).wait_send()
            out_arrived(z, k).wait()

        return carry

    lax.fori_loop(0, PLANES * CHIPS, drain_out, 0)

    def drain_feat(k, carry):
        for g in range(len(PARTS)):
            feat_copy(g, k).wait_send()
        return carry

    lax.fori_loop(1, CHIPS, drain_feat, 0)
    for i in range(OWN):
        for k in range(1, SIDE):
            tap_copy1(i, k).wait_send()
            tap_copy2(i, k).wait_send()
    for c in range(len(COUPLES)):
        tap_copy3(c).wait_send()
    bottom.wait_send()
    top.wait_send()
    middle.wait_send()

    @pl.when(slab > 0)
    def _():
        down.wait_send()
        low.wait_send()

    @pl.when(slab < slabs - 1)
    def _():
        up.wait_send()
        high.wait_send()


def body(features, weights, bias_vector):
    DMA = pltpu.SemaphoreType.DMA
    hbm = pl.BlockSpec(memory_space=pltpu.HBM)
    anywhere = pl.BlockSpec(memory_space=pl.ANY)
    flat = weights.reshape(9, 3, 8, 256)
    got = pl.pallas_call(
        kernel,
        out_shape=jax.ShapeDtypeStruct((PLANES, 64, 8, 128), jnp.bfloat16),
        in_specs=[hbm, hbm, hbm],
        out_specs=anywhere,
        scratch_shapes=[
            pltpu.VMEM((PLANES, 8, 64, 128), jnp.bfloat16),
            pltpu.VMEM((256,), jnp.float32),
            pltpu.VMEM((66, PLANES, 8, 128), jnp.bfloat16),
            pltpu.VMEM((ROWS + 2, PLANES + 2, CHIPS, 2, 8, 128), jnp.bfloat16),
            pltpu.VMEM((9, 3, SIDE, SIDE, 8, 256), jnp.bfloat16),
            pltpu.VMEM((PLANES, 384, ROWS * 128), jnp.float32),
            pltpu.VMEM((PLANES, CHIPS, ROWS, 8, 128), jnp.bfloat16),
            pltpu.VMEM((CHIPS, 2, 8, 128), jnp.float32),
            DMA((len(PARTS), CHIPS)), DMA((len(PARTS), CHIPS)),
            DMA((5,)), DMA((5,)),
            DMA((2,)), DMA((2,)),
            DMA((OWN, SIDE)), DMA((OWN, SIDE)),
            DMA((OWN, SIDE)), DMA((OWN, SIDE)),
            DMA((len(COUPLES),)), DMA((len(COUPLES),)),
            DMA((PLANES, CHIPS)), DMA((PLANES, CHIPS)),
            DMA((3 + OWN,)),
        ],
        compiler_params=pltpu.CompilerParams(
            collective_id=0, has_side_effects=True, vmem_limit_bytes=40 * 1024 * 1024
        ),
    )(*[pltpu.with_memory_space_constraint(a, pltpu.HBM) for a in (features, flat, bias_vector)])
    return got.transpose(0, 2, 1, 3)


def solution(mesh):
    placed = (P("slab", "filt", None, None), P(None, None, None, "filt", None), P())
    return jax.shard_map(
        body, mesh=mesh, in_specs=placed, out_specs=P("slab", "filt", None, None), check_vma=False
    )
```

```python
import jax
import jax.numpy as jnp
from jax import lax
from jax.experimental import pallas as pl
from jax.experimental.pallas import tpu as pltpu
from jax.sharding import PartitionSpec as P

MESH = pl.DeviceIdType.MESH
SIDE = 4
CHIPS = 16
ROWS = 4
PLANES = 4
COUPLES = ((0, 6), (2, 8))
COMMON = (3, 4, 5, 1, 7)
OWN = len(COUPLES) + len(COMMON)
X_FIRST = (1, 3, 5)
PARTS = (0, 3, slice(1, 3))
PLACES = (1, 4, slice(2, 4))
FAR = (10, 6, 9, 14, 11, 2, 8, 5, 15, 7, 13, 1, 4, 3, 12)


def kernel(feat_hbm, w, bias_hbm, out, feat, bias, turned, vol, taps, acc, ready, column,
           f_s, f_r, x_s, x_r, h_s, h_r, w1_s, w1_r, w2_s, w2_r, z_s, z_r, o_s, o_r, l_s):
    slab = lax.axis_index("slab")
    filt = lax.axis_index("filt")
    slabs = lax.axis_size("slab")
    chip = filt // 2
    core = filt % 2
    cy = chip // SIDE
    cx = chip % SIDE

    def device(y, x, c):
        return {"filt": (y * SIDE + x) * 2 + c}

    def partner(k):
        y = (cy + k // SIDE) % SIDE
        x = (cx + k % SIDE) % SIDE
        return y, x

    def source(k):
        y = (cy + SIDE - k // SIDE) % SIDE
        x = (cx + SIDE - k % SIDE) % SIDE
        return y * SIDE + x

    barrier = pltpu.get_barrier_semaphore()

    def greet(k, carry):
        y, x = partner(k)
        pl.semaphore_signal(barrier, inc=1, device_id=device(y, x, core), device_id_type=MESH)
        return carry

    lax.fori_loop(1, CHIPS, greet, 0)
    pl.semaphore_signal(barrier, inc=1, device_id=device(cy, cx, 1 - core), device_id_type=MESH)

    for step in (1, slabs - 1):
        pl.semaphore_signal(
            barrier, inc=1, device_id={"slab": (slab + step) % slabs}, device_id_type=MESH
        )

    odd = slab % 2

    def pair(i, parity):
        if i >= len(COUPLES):
            return COMMON[i - len(COUPLES)]
        first, second = COUPLES[i]
        return first + parity * (second - first)

    take_feat = pltpu.make_async_copy(feat_hbm, feat, l_s.at[0])
    take_feat.start()
    take_bias = pltpu.make_async_copy(bias_hbm, bias, l_s.at[1])
    take_bias.start()
    own_taps = []
    for i in range(OWN):
        unit = pair(i, odd)
        own_taps.append(pltpu.make_async_copy(w.at[unit], taps.at[unit, :, cy, cx], l_s.at[3 + i]))
        own_taps[i].start()

    @pl.when(slab == 0)
    def _():
        for y in range(ROWS + 2):
            vol[y, 0] = jnp.zeros(vol.shape[2:], vol.dtype)

    @pl.when(slab == slabs - 1)
    def _():
        for y in range(ROWS + 2):
            vol[y, 5] = jnp.zeros(vol.shape[2:], vol.dtype)

    turned[0] = jnp.zeros(turned.shape[1:], turned.dtype)
    turned[turned.shape[0] - 1] = jnp.zeros(turned.shape[1:], turned.dtype)
    take_feat.wait()
    for z in range(PLANES):
        turned[1:65, z] = jnp.transpose(feat[z].astype(jnp.float32), (1, 0, 2)).astype(jnp.bfloat16)

    own_feat = pltpu.make_async_copy(
        turned.at[pl.ds(chip * ROWS, ROWS + 2)], vol.at[:, 1:5, chip, core], l_s.at[2]
    )
    own_feat.start()

    take_bias.wait()
    wide = jnp.broadcast_to(bias[...].reshape(1, 256), (128, 256))
    column[...] = jnp.transpose(wide, (1, 0)).reshape(CHIPS, 2, 8, 128)

    pl.semaphore_wait(barrier, CHIPS + 2)

    def feat_copy(g, k):
        y, x = partner(k)
        return pltpu.make_async_remote_copy(
            src_ref=turned.at[pl.ds((y * SIDE + x) * ROWS, ROWS + 2), PARTS[g]],
            dst_ref=vol.at[:, PLACES[g], chip, core],
            send_sem=f_s.at[g, k], recv_sem=f_r.at[g, k],
            device_id=device(y, x, core), device_id_type=MESH,
        )

    def send_feat(g):
        for k in FAR:
            feat_copy(g, k).start()

    def wait_feat(g):
        def wait(k, carry):
            piece = vol.at[:, PLACES[g], source(k), core]
            pltpu.make_async_copy(piece, piece, f_r.at[g, k]).wait()
            return carry

        lax.fori_loop(1, CHIPS, wait, 0)

    def ring(i, k, phase, sign):
        step = k if sign > 0 else SIDE - k
        if (i in X_FIRST) == (phase == 1):
            return cy, (cx + step) % SIDE
        return (cy + step) % SIDE, cx

    def tap_copy1(i, k):
        y, x = ring(i, k, 1, 1)
        return pltpu.make_async_remote_copy(
            src_ref=w.at[pair(i, odd)], dst_ref=taps.at[pair(i, odd), :, cy, cx],
            send_sem=w1_s.at[i, k], recv_sem=w1_r.at[i, k],
            device_id=device(y, x, core), device_id_type=MESH,
        )

    def tap_arrived1(i, k):
        y, x = ring(i, k, 1, -1)
        piece = taps.at[pair(i, odd), :, y, x]
        return pltpu.make_async_copy(piece, piece, w1_r.at[i, k])

    def tap_line(i, y, x):
        if i in X_FIRST:
            return taps.at[pair(i, odd), :, y]
        return taps.at[pair(i, odd), :, :, x]

    def tap_copy2(i, k):
        y, x = ring(i, k, 2, 1)
        line = tap_line(i, cy, cx)
        return pltpu.make_async_remote_copy(
            src_ref=line, dst_ref=line, send_sem=w2_s.at[i, k], recv_sem=w2_r.at[i, k],
            device_id=device(y, x, core), device_id_type=MESH,
        )

    def tap_arrived2(i, k):
        y, x = ring(i, k, 2, -1)
        line = tap_line(i, y, x)
        return pltpu.make_async_copy(line, line, w2_r.at[i, k])

    def tap_copy3(c):
        unit = taps.at[pair(c, odd)]
        step = 1 if c == 0 else slabs - 1
        return pltpu.make_async_remote_copy(
            src_ref=unit, dst_ref=unit, send_sem=z_s.at[c], recv_sem=z_r.at[c],
            device_id={"slab": (slab + step) % slabs}, device_id_type=MESH,
        )

    def tap_arrived3(c):
        unit = taps.at[pair(c, 1 - odd)]
        return pltpu.make_async_copy(unit, unit, z_r.at[c])

    def second_phase(which):
        for i in which:
            own_taps[i].wait()
            for k in range(1, SIDE):
                tap_arrived1(i, k).wait()
            for k in (2, 1, 3):
                tap_copy2(i, k).start()

    def third_phase():
        for c in range(len(COUPLES)):
            for k in range(1, SIDE):
                tap_arrived2(c, k).wait()
            tap_copy3(c).start()

    def across(index, part):
        return pltpu.make_async_remote_copy(
            src_ref=part, dst_ref=part, send_sem=x_s.at[index], recv_sem=x_r.at[index],
            device_id=device(cy, cx, 1 - core), device_id_type=MESH,
        )

    def across_arrived(index, part):
        return pltpu.make_async_copy(part, part, x_r.at[index])

    down = pltpu.make_async_remote_copy(
        src_ref=vol.at[:, 1, :, core], dst_ref=vol.at[:, 5, :, core],
        send_sem=h_s.at[0], recv_sem=h_r.at[0],
        device_id={"slab": slab - 1}, device_id_type=MESH,
    )
    up = pltpu.make_async_remote_copy(
        src_ref=vol.at[:, 4, :, core], dst_ref=vol.at[:, 0, :, core],
        send_sem=h_s.at[1], recv_sem=h_r.at[1],
        device_id={"slab": slab + 1}, device_id_type=MESH,
    )

    send_feat(0)
    send_feat(1)
    for i in range(OWN):
        for k in range(1, SIDE):
            tap_copy1(i, k).start()
    send_feat(2)
    second_phase(range(len(COUPLES)))
    own_feat.wait()
    wait_feat(0)

    @pl.when(slab > 0)
    def _():
        down.start()

    bottom = across(0, vol.at[:, 1, :, core])
    bottom.start()
    wait_feat(1)

    @pl.when(slab < slabs - 1)
    def _():
        up.start()

    top = across(3, vol.at[:, 4, :, core])
    top.start()
    second_phase(range(len(COUPLES), OWN))
    wait_feat(2)
    middle = across(4, vol.at[:, 2:4, :, core])
    middle.start()
    third_phase()

    low = across(1, vol.at[:, 0, :, core])
    high = across(2, vol.at[:, 5, :, core])
    across_arrived(0, vol.at[:, 1, :, 1 - core]).wait()
    across_arrived(3, vol.at[:, 4, :, 1 - core]).wait()
    across_arrived(4, vol.at[:, 2:4, :, 1 - core]).wait()

    lane = lax.broadcasted_iota(jnp.int32, (128, 128), 1)

    def out_copy(z, k):
        y, x = partner(k)
        return pltpu.make_async_remote_copy(
            src_ref=ready.at[z, y * SIDE + x], dst_ref=out.at[z, pl.ds(chip * ROWS, ROWS)],
            send_sem=o_s.at[z, k], recv_sem=o_r.at[z, k],
            device_id=device(y, x, core), device_id_type=MESH,
        )

    def out_arrived(z, k):
        piece = out.at[z, pl.ds(source(k) * ROWS, ROWS)]
        return pltpu.make_async_copy(piece, piece, o_r.at[z, k])

    def out_own(z):
        return pltpu.make_async_copy(
            ready.at[z, chip], out.at[z, pl.ds(chip * ROWS, ROWS)], o_s.at[z, 0]
        )

    def finish(z):
        biases = column[:, core].reshape(128, 128)
        for y in range(ROWS):
            part = acc[z, :, y * 128 : (y + 1) * 128]
            before = jnp.where(lane == 0, 0.0, pltpu.roll(part[0:128], 1, 1))
            after = jnp.where(lane == 127, 0.0, pltpu.roll(part[256:384], 127, 1))
            shifted = before + part[128:256] + after + biases
            active = jnp.where(shifted > 0, shifted, 0.3 * shifted)
            ready[z, :, y] = active.reshape(CHIPS, 8, 128).astype(jnp.bfloat16)
        out_own(z).start()

        for k in FAR:
            out_copy(z, k).start()

    def multiply(unit, first=False, last=False):
        dz, dy = unit // 3, unit % 3
        lines = [
            vol[dy + y, z + dz].reshape(256, 128) for z in range(PLANES) for y in range(ROWS)
        ]
        product = jnp.dot(
            taps[unit].reshape(384, 256),
            jnp.concatenate(lines, axis=1),
            preferred_element_type=jnp.float32,
        )
        for z in range(PLANES):
            part = product[:, z * ROWS * 128 : (z + 1) * ROWS * 128]
            if first:
                acc[z] = part
            else:
                acc[z] += part
            if last:
                finish(z)

    for i in range(len(COUPLES), OWN):
        for k in range(1, SIDE):
            tap_arrived2(i, k).wait()
        if i == len(COUPLES) + 1:
            @pl.when(slab > 0)
            def _():
                edge = vol.at[:, 0, :, core]
                pltpu.make_async_copy(edge, edge, h_r.at[1]).wait()
                low.start()

            @pl.when(slab < slabs - 1)
            def _():
                edge = vol.at[:, 5, :, core]
                pltpu.make_async_copy(edge, edge, h_r.at[0]).wait()
                high.start()

        if i == len(COUPLES) + 3:
            @pl.when(slab > 0)
            def _():
                across_arrived(1, vol.at[:, 0, :, 1 - core]).wait()

            @pl.when(slab < slabs - 1)
            def _():
                across_arrived(2, vol.at[:, 5, :, 1 - core]).wait()

        if i == OWN - 1:
            for c in range(len(COUPLES)):
                tap_arrived3(c).wait()
                multiply(COUPLES[c][0])
                multiply(COUPLES[c][1])
        multiply(pair(i, 0), first=i == len(COUPLES), last=i == OWN - 1)

    def drain_out(i, carry):
        z = i // CHIPS
        k = i % CHIPS

        @pl.when(k == 0)
        def _():
            out_own(z).wait()

        @pl.when(k > 0)
        def _():
            out_copy(z, k).wait_send()
            out_arrived(z, k).wait()

        return carry

    lax.fori_loop(0, PLANES * CHIPS, drain_out, 0)

    def drain_feat(k, carry):
        for g in range(len(PARTS)):
            feat_copy(g, k).wait_send()
        return carry

    lax.fori_loop(1, CHIPS, drain_feat, 0)
    for i in range(OWN):
        for k in range(1, SIDE):
            tap_copy1(i, k).wait_send()
            tap_copy2(i, k).wait_send()
    for c in range(len(COUPLES)):
        tap_copy3(c).wait_send()
    bottom.wait_send()
    top.wait_send()
    middle.wait_send()

    @pl.when(slab > 0)
    def _():
        down.wait_send()
        low.wait_send()

    @pl.when(slab < slabs - 1)
    def _():
        up.wait_send()
        high.wait_send()


def body(features, weights, bias_vector):
    DMA = pltpu.SemaphoreType.DMA
    hbm = pl.BlockSpec(memory_space=pltpu.HBM)
    anywhere = pl.BlockSpec(memory_space=pl.ANY)
    flat = weights.reshape(9, 3, 8, 256)
    got = pl.pallas_call(
        kernel,
        out_shape=jax.ShapeDtypeStruct((PLANES, 64, 8, 128), jnp.bfloat16),
        in_specs=[hbm, hbm, hbm],
        out_specs=anywhere,
        scratch_shapes=[
            pltpu.VMEM((PLANES, 8, 64, 128), jnp.bfloat16),
            pltpu.VMEM((256,), jnp.float32),
            pltpu.VMEM((66, PLANES, 8, 128), jnp.bfloat16),
            pltpu.VMEM((ROWS + 2, PLANES + 2, CHIPS, 2, 8, 128), jnp.bfloat16),
            pltpu.VMEM((9, 3, SIDE, SIDE, 8, 256), jnp.bfloat16),
            pltpu.VMEM((PLANES, 384, ROWS * 128), jnp.float32),
            pltpu.VMEM((PLANES, CHIPS, ROWS, 8, 128), jnp.bfloat16),
            pltpu.VMEM((CHIPS, 2, 8, 128), jnp.float32),
            DMA((len(PARTS), CHIPS)), DMA((len(PARTS), CHIPS)),
            DMA((5,)), DMA((5,)),
            DMA((2,)), DMA((2,)),
            DMA((OWN, SIDE)), DMA((OWN, SIDE)),
            DMA((OWN, SIDE)), DMA((OWN, SIDE)),
            DMA((len(COUPLES),)), DMA((len(COUPLES),)),
            DMA((PLANES, CHIPS)), DMA((PLANES, CHIPS)),
            DMA((3 + OWN,)),
        ],
        compiler_params=pltpu.CompilerParams(
            collective_id=0, has_side_effects=True, vmem_limit_bytes=40 * 1024 * 1024
        ),
    )(*[pltpu.with_memory_space_constraint(a, pltpu.HBM) for a in (features, flat, bias_vector)])
    return got.transpose(0, 2, 1, 3)


def solution(mesh):
    placed = (P("slab", "filt", None, None), P(None, None, None, "filt", None), P())
    return jax.shard_map(
        body, mesh=mesh, in_specs=placed, out_specs=P("slab", "filt", None, None), check_vma=False
    )
```
